32 devices in a mesh: ctx: 8 (over y, x, core), hs: 4 (over z).
Axes of the slice: x: 2, y: 2, z: 4, core: 2. Of those that a mesh axis runs over, the one named last changes fastest.
Arguments:
- queries: bfloat16 [4, 8192, 512], P('hs', 'ctx'), may hold values from -40 to 40
- keys: bfloat16 [4, 8192, 512], P('hs', 'ctx'), may hold values from -6 to 6
- values: bfloat16 [4, 8192, 512], P('hs', 'ctx'), may hold values from -6 to 6
- rates: float32 [4, 8192], P('hs', 'ctx'), may hold values from 0.02 to 0.2
- doc_ids: int32 [2, 8192], replicated, may hold values from 0 to 3, never falling along the last dimension, each value on 1 to 4096 neighbouring positions
- fast_weights: bfloat16 [4, 3, 512, 512], P('hs'), may hold values from -0.25 to 0.25
- momentum: float32 [4, 3, 512, 512], P('hs'), may hold values from -0.2 to 0.2
- head_gain: float32 [4, 512], P('hs'), may hold values from 0.5 to 2
Outputs:
- tokens_out: bfloat16 [4, 8192, 512], P('hs', 'ctx')
- new_weights: bfloat16 [4, 3, 512, 512], P('hs')
The draws below stay inside these ranges and needn't reach their ends.
Inputs may be any that keep to these rules, and one draw needn't show every extreme that they name: `doc_ids`: each row never falls; a document has at most 4096 positions and some document has exactly that many.
All inputs are finite; a program needn't handle non-finite values.
Results may differ from the reference program's by a relative error of at most 0.0092.
Values may be sent and summed in bfloat16 or wider, within the bound.
A program may use at most 64 MiB of HBM per device.

```python
import math
import jax
import jax.numpy as jnp
import numpy as np
from jax import lax

DH = 512
FH = 512
WINDOW_TOKENS = 512
SEQS = 2
TOKENS = 8192
PAIRS = 4
HEADS = 2


def joint_draw(key):
    base = jax.random.fold_in(key, 911)
    first, second = jax.random.split(base, 2)
    shape = (PAIRS, TOKENS, DH)
    keyset = jnp.clip(jax.random.normal(first, shape, jnp.float32), -4.0, 4.0)
    queryset = jnp.clip(jax.random.normal(second, shape, jnp.float32), -4.0, 4.0)
    return (queryset, keyset)


def draw_queries(key, part):
    return joint_draw(key)[0].astype(jnp.bfloat16)


def draw_keys(key, part):
    return joint_draw(key)[1].astype(jnp.bfloat16)


def block_scale(stream_key, dims, shards, low, top_value):
    def one(position, shards_of):
        draws = jax.random.uniform(jax.random.fold_in(jax.random.fold_in(stream_key, 6), position), (shards_of,), jnp.float32, low / len(shards), top_value / len(shards))
        return jnp.repeat(jnp.exp(draws), dims[position] // shards_of).reshape((-1,) + (1,) * (len(dims) - position - 1))

    loudness = one(*shards[0])
    for cut in shards[1:]:
        loudness = loudness * one(*cut)
    return loudness


def profile(number_of, total, reach, skew):
    portions = [(1 << 20) // math.isqrt(grade ** skew) + 1 for grade in range(2, number_of + 1)]
    rest, holding = total - reach - (number_of - 1), [1] * (number_of - 1)
    while rest > 0:
        candidates = [i for i in range(number_of - 1) if holding[i] < reach]
        mass, budget = sum([portions[i] for i in candidates]), rest
        for i in candidates:
            extra = min(reach - holding[i], max(1, budget * portions[i] // mass), rest)
            holding[i] = holding[i] + extra
            rest = rest - extra
    return np.array([reach] + holding)


def ragged_sizes(rng, number_of, total, limit, lean):
    if number_of == 2:
        one = jax.random.randint(rng, (), max(1, total - limit), min(limit, total - 1) + 1)
        return jnp.stack([one, total - one])
    tallies = jnp.asarray(profile(number_of, total, limit, lean), jnp.int32)
    pairs = (number_of - 1) // 2
    donor, receiver = tallies[1:1 + 2 * pairs:2], tallies[2:2 + 2 * pairs:2]
    margin = jnp.minimum(donor - 1, limit - receiver)
    shifted = jax.random.randint(jax.random.fold_in(rng, 1), (pairs,), 0, 1 << 20) % (margin + 1)
    tallies = tallies.at[1:1 + 2 * pairs:2].set(donor - shifted).at[2:2 + 2 * pairs:2].set(receiver + shifted)
    return tallies[jax.random.permutation(jax.random.fold_in(rng, 2), number_of)]


def bell_draw(key, shape, spread, reach, shards=(), held_as=jnp.bfloat16):
    level = block_scale(key, shape, shards, -0.22, 0.18) if shards else 1.0
    values = jax.random.normal(key, shape, jnp.float32) * spread * level
    return jnp.minimum(jnp.maximum(values, -reach), reach).astype(held_as)


def setup_inputs(seed: int = 0) -> dict:
    seeds = jax.random.split(jax.random.key(seed), 9)
    queries = draw_queries(jax.random.fold_in(seeds[8], 71), 0)
    keys = draw_keys(jax.random.fold_in(seeds[8], 71), 0)
    values = bell_draw(seeds[2], (PAIRS, TOKENS, DH), 1.0, 6.0, ((0, 4), (1, 8)))
    rates = jnp.clip(jnp.exp(math.log(0.2) - 2.3025851 * jax.random.uniform(seeds[3], (PAIRS, TOKENS), jnp.float32) ** block_scale(seeds[3], (PAIRS, TOKENS), ((0, 4), (1, 8)), -0.2, 0.2)), 0.02, 0.2)
    doc_ids = jax.vmap(lambda own: jnp.searchsorted(jnp.cumsum(ragged_sizes(own, 4, TOKENS, TOKENS // 2, 1)), jnp.arange(TOKENS), side="right"))(jax.random.split(seeds[4], SEQS)).reshape((SEQS, TOKENS)).astype(jnp.int32)
    fast_weights = bell_draw(seeds[5], (PAIRS, 3, DH, FH), DH ** -0.5, 0.25, ((0, 4),))
    momentum = bell_draw(seeds[6], (PAIRS, 3, DH, FH), 0.03, 0.2, ((0, 4),), jnp.float32)
    head_gain = jnp.clip(jnp.exp(math.log(2.0) - 1.3862944 * jax.random.uniform(seeds[7], (PAIRS, DH), jnp.float32) ** block_scale(seeds[7], (PAIRS, DH), ((0, 4),), -0.2, 0.2)), 0.5, 2.0)
    return dict(queries=queries, keys=keys, values=values, rates=rates, doc_ids=doc_ids, fast_weights=fast_weights, momentum=momentum, head_gain=head_gain)


def attend_block(qb, kb, value_block, qpos, kpos, qdoc, kdoc):
    scores = jnp.einsum('qd,kd->qk', qb, kb, preferred_element_type=jnp.float32) / math.sqrt(qb.shape[1])
    valid = (kpos[None, :] <= qpos[:, None]) & (kpos[None, :] > qpos[:, None] - WINDOW_TOKENS) & (kpos[None, :] >= 0) & (kdoc[None, :] == qdoc[:, None])
    scores = jnp.where(valid, scores, -1e+30)
    top = lax.optimization_barrier(jnp.max(scores, axis=1, keepdims=True))
    expo = jnp.where(valid, jnp.exp(scores - top), 0.0)
    probs = (expo / lax.optimization_barrier(jnp.sum(expo, axis=1, keepdims=True))).astype(jnp.bfloat16)
    return jnp.dot(probs, value_block, preferred_element_type=jnp.float32)

def renew(weights, mom_old, grads):
    mom = 0.9 * mom_old + grads
    wf = weights.astype(jnp.float32)
    cand = wf - mom
    old_rms = jnp.sqrt(lax.optimization_barrier(jnp.mean(wf * wf, axis=1, keepdims=True)) + 1e-06)
    new_rms = jnp.sqrt(lax.optimization_barrier(jnp.mean(cand * cand, axis=1, keepdims=True)) + 1e-06)
    return (cand * old_rms / new_rms).astype(jnp.bfloat16)

def one_pair(packed):
    qrow, krow, value_row_index, lrow, weights, mom_old, docrow = packed
    zeroed_rows = jnp.zeros((WINDOW_TOKENS, DH), jnp.bfloat16)
    kpad = jnp.concatenate([zeroed_rows, krow], axis=0)
    value_padded = jnp.concatenate([zeroed_rows, value_row_index], axis=0)
    dpad = jnp.concatenate([jnp.zeros((WINDOW_TOKENS,), jnp.int32), docrow], axis=0)

    def block(index):
        begin_offset = (index * WINDOW_TOKENS).astype(jnp.int32)
        qb = lax.dynamic_slice_in_dim(qrow, begin_offset, WINDOW_TOKENS, 0)
        kb = lax.dynamic_slice_in_dim(kpad, begin_offset, 2 * WINDOW_TOKENS, 0)
        value_block = lax.dynamic_slice_in_dim(value_padded, begin_offset, 2 * WINDOW_TOKENS, 0)
        qpos = begin_offset + jnp.arange(WINDOW_TOKENS, dtype=jnp.int32)
        kpos = begin_offset - WINDOW_TOKENS + jnp.arange(2 * WINDOW_TOKENS, dtype=jnp.int32)
        qdoc = lax.dynamic_slice_in_dim(docrow, begin_offset, WINDOW_TOKENS, 0)
        kdoc = lax.dynamic_slice_in_dim(dpad, begin_offset, 2 * WINDOW_TOKENS, 0)
        return attend_block(qb, kb, value_block, qpos, kpos, qdoc, kdoc)
    attn = lax.map(block, jnp.arange(TOKENS // WINDOW_TOKENS, dtype=jnp.int32)).reshape(TOKENS, DH)
    h1 = jnp.dot(krow, weights[0], preferred_element_type=jnp.float32)
    h3 = jnp.dot(krow, weights[1], preferred_element_type=jnp.float32)
    act = jax.nn.silu(h1)
    gk = (act * h3).astype(jnp.bfloat16)
    scaled = (lrow[:, None] * value_row_index.astype(jnp.float32) / math.sqrt(TOKENS)).astype(jnp.bfloat16)
    dg = -jnp.dot(scaled, weights[2], preferred_element_type=jnp.float32)
    sig = jax.nn.sigmoid(h1)
    dh1 = (dg * h3 * sig * (1.0 + h1 * (1.0 - sig))).astype(jnp.bfloat16)
    dh3 = (dg * act).astype(jnp.bfloat16)
    g_one = jnp.einsum('td,tf->df', krow, dh1, preferred_element_type=jnp.float32)
    g_three = jnp.einsum('td,tf->df', krow, dh3, preferred_element_type=jnp.float32)
    g_down = -jnp.einsum('td,tf->df', scaled, gk, preferred_element_type=jnp.float32)
    grads = jnp.stack([g_one, g_three, g_down])
    fresh = renew(weights, mom_old, grads)
    o_one = jnp.dot(qrow, fresh[0], preferred_element_type=jnp.float32)
    o_three = jnp.dot(qrow, fresh[1], preferred_element_type=jnp.float32)
    gq = (jax.nn.silu(o_one) * o_three).astype(jnp.bfloat16)
    fast_out = jnp.einsum('tf,df->td', gq, fresh[2], preferred_element_type=jnp.float32)
    return (attn + fast_out, fresh)

def reference(queries, keys, values, rates, doc_ids, fast_weights, momentum, head_gain):
    pair_seq = (jnp.arange(PAIRS, dtype=jnp.int32) // HEADS).astype(jnp.int32)
    docrows = doc_ids[pair_seq]
    mixed, fresh = lax.map(one_pair, (queries, keys, values, rates, fast_weights, momentum, docrows))
    squares = lax.optimization_barrier(jnp.sum(mixed * mixed, axis=2)).reshape(SEQS, HEADS, TOKENS)
    totals = lax.optimization_barrier(jnp.sum(squares, axis=1))
    scale_rows = 1.0 / jnp.sqrt(totals / (HEADS * DH) + 1e-06)

    def normalize(packed):
        yrow, gain, seq = packed
        srow = lax.dynamic_index_in_dim(scale_rows, seq, 0, keepdims=False)
        return (yrow * srow[:, None] * gain[None, :]).astype(jnp.bfloat16)
    tokens_out = lax.map(normalize, (mixed, head_gain, pair_seq))
    return (tokens_out, fresh)
```

```python
import functools
import math

import jax
import jax.numpy as jnp
from jax import lax
from jax.experimental import pallas as pl
from jax.experimental.pallas import tpu as pltpu
from jax.sharding import PartitionSpec as P

WINDOW_TOKENS = 512
BLOCK = 256
QBLOCK = 512
MESH = pl.DeviceIdType.MESH
F32 = jnp.float32
PLAN = (
    "|", "F", "F", "F", "F", "g4", "g5", "B0", "g0", "4", "g2", "B1", "5", "g1", "0", "4", "g3",
    "2", "5", "P4", "P5", "D", "Q", "0", "E", "4", "V", "1", "2", "5", "V", "3", "P0", "P2", "0",
    "V", "4", "1", "E", "2", "V", "5", "3", "P1", "P3", "K", "0", "4", "S", "1", "V", "2", "5", "3",
    "V", "4", "0", "S", "1", "V", "5", "2", "3", "V", "0", "2", "O0", "1", "M0", "r", "3", "W0",
    "1", "O1", "r", "3", "M1",
)
FIRST = ("xy", "xy", "xy", "xy", "xy", "xy",)
SPLIT = 2
PIECES = 8
BF16 = jnp.bfloat16


def as_column(row):
    return jnp.transpose(jnp.broadcast_to(row, (128, row.shape[1])), (1, 0))


def kernel(
    n, heads, seqs,
    q_hbm, k_hbm, v_hbm, rates_hbm, doc_hbm, w_hbm, mom_hbm, gain_hbm,
    y, wt, ss_out, gain_out,
    q, kx, vx, w, mom, docs, rates, dh, u, acc, sbuf, rbuf, cand, base, old_rms, hold,
    gq, held, norms, ss_own, ss_got, doc_cols,
    k_sem, v_sem, w_sem, local_sem, halo_send, halo_recv,
    rs_send, rs_recv, ag_send, ag_recv, ss_send, ss_recv,
):
    rows, width = q.shape
    win = WINDOW_TOKENS
    wrows = w.shape[1]
    phases = n.bit_length() - 1
    blocks = rows // BLOCK
    me = lax.axis_index("ctx")
    hs = lax.axis_index("hs")
    seq = hs // heads
    head_base = seq * heads
    peers = [head_base + (hs - head_base + d) % heads for d in range(1, heads)]
    offset = me * rows
    before = jnp.maximum(me * rows - win, 0)

    bits = [(me // (1 << i)) % 2 for i in range(phases)]
    core = bits[0]
    orders = {"x": list(range(phases)), "y": [0] + list(range(phases - 1, 0, -1))}
    chunks = 3 * SPLIT
    crows = wrows // SPLIT
    own = crows >> phases
    partner, keep, drop, low = [], [], [], []
    for c in range(chunks):
        mine_first, other_first = orders[FIRST[c][0]], orders[FIRST[c][1]]
        partner.append([])
        keep.append([])
        drop.append([])
        at = (c % SPLIT) * crows
        for j in range(phases):
            a, b = mine_first[j], other_first[j]
            bit = bits[a] if a == b else bits[a] * (1 - core) + bits[b] * core
            stride = (1 << a) if a == b else (1 << a) * (1 - core) + (1 << b) * core
            half = crows >> (j + 1)
            partner[c].append(me + (1 - 2 * bit) * stride)
            keep[c].append(at + bit * half)
            drop[c].append(at + (1 - bit) * half)
            at = at + bit * half
        low.append(at)

    def at_rows(start, size):
        return pl.ds(pl.multiple_of(start, size), size)

    lanes_own = [pl.ds(pl.multiple_of((at // 128) * 128, 128), 128) for at in low]
    within = [at_rows(at - (at // 128) * 128, own) for at in low]

    def block_at(i, start=0):
        return pl.ds(start + i * BLOCK, BLOCK)

    k_loads = [pltpu.make_async_copy(k_hbm.at[block_at(i)], kx.at[block_at(i, win)], k_sem.at[i])
               for i in range(blocks)]
    v_loads = [pltpu.make_async_copy(v_hbm.at[block_at(i)], vx.at[block_at(i, win)], v_sem.at[i])
               for i in range(blocks)]
    w_loads = [pltpu.make_async_copy(w_hbm.at[c], w.at[c], w_sem.at[c]) for c in range(3)]
    doc_loads = [
        pltpu.make_async_copy(
            doc_hbm.at[:, pl.ds(pl.multiple_of(before, 128), win)],
            docs.at[:, pl.ds(0, win)], local_sem.at[0]),
        pltpu.make_async_copy(
            doc_hbm.at[:, pl.ds(pl.multiple_of(offset, 128), rows)],
            docs.at[:, pl.ds(win, rows)], local_sem.at[1]),
    ]
    rate_load = pltpu.make_async_copy(rates_hbm, rates, local_sem.at[2])
    gain_load = pltpu.make_async_copy(gain_hbm, gain_out, local_sem.at[3])
    q_load = pltpu.make_async_copy(q_hbm, q, local_sem.at[4])
    mom_loads = [pltpu.make_async_copy(mom_hbm.at[c // SPLIT, :, lanes_own[c]], mom.at[c], local_sem.at[5 + c])
                 for c in range(chunks)]

    barrier = pltpu.get_barrier_semaphore()
    for d in range(1, n):
        pl.semaphore_signal(barrier, 1, device_id={"ctx": (me + d) % n}, device_id_type=MESH)
    for peer in peers:
        pl.semaphore_signal(barrier, 1, device_id={"hs": peer}, device_id_type=MESH)

    for load in [k_loads[0], w_loads[0], w_loads[1], rate_load, v_loads[0], k_loads[1], v_loads[1]]:
        load.start()

    piece = win // PIECES
    halo = [[
        pltpu.make_async_remote_copy(
            src_ref=src.at[pl.ds(rows - win + p * piece, piece)], dst_ref=dst.at[pl.ds(p * piece, piece)],
            send_sem=halo_send.at[i, p], recv_sem=halo_recv.at[i, p],
            device_id={"ctx": (me + 1) % n}, device_id_type=MESH,
        ) for p in range(PIECES)]
        for i, (src, dst) in enumerate(((k_hbm, kx), (v_hbm, vx)))
    ]

    def halo_start(i, p):
        @pl.when(me < n - 1)
        def _():
            halo[i][p].start()

    def meet():
        pl.semaphore_wait(barrier, n - 1 + len(peers))
        for p in range(PIECES):
            halo_start(0, p)

    @pl.when(me == 0)
    def _():
        kx[0:win, :] = jnp.zeros((win, width), BF16)
        vx[0:win, :] = jnp.zeros((win, width), BF16)

    total = rows * n
    done = {"F": 0}

    def forward():
        i = done["F"]
        done["F"] += 1
        if i == 0:
            for load in [k_loads[0], w_loads[0], w_loads[1], rate_load, v_loads[0]]:
                load.wait()
            for b in range(2, blocks):
                k_loads[b].start()
                v_loads[b].start()
            w_loads[2].start()
        else:
            k_loads[i].wait()
            v_loads[i].wait()
        if i == blocks - 1:
            for load in doc_loads + [q_load] + mom_loads + [gain_load]:
                load.start()
        at = block_at(i)
        kb = kx[block_at(i, win), :]
        h1 = jnp.dot(kb, w[0], preferred_element_type=F32)
        h3 = jnp.dot(kb, w[1], preferred_element_type=F32)
        vb = vx[block_at(i, win), :].astype(F32)
        rate = as_column(rates[:, at])[:, :1]
        u[at, :] = (rate * vb * (-1.0 / math.sqrt(total))).astype(BF16)
        sig = 1.0 / (1.0 + jnp.exp(-h1))
        act = h1 * sig
        dh[2, at, :] = (act * h3).astype(BF16)
        hold[0, at, :] = h3 * sig * (1.0 + h1 * (1.0 - sig))
        hold[1, at, :] = act

    def slot(c, j):
        return pl.ds((c % SPLIT) * crows + crows - (crows >> j), crows >> (j + 1))

    def scatter(c, j):
        return pltpu.make_async_remote_copy(
            src_ref=sbuf.at[c // SPLIT, slot(c, j), :], dst_ref=rbuf.at[c // SPLIT, slot(c, j), :],
            send_sem=rs_send.at[c, j], recv_sem=rs_recv.at[c, j],
            device_id={"ctx": partner[c][j]}, device_id_type=MESH)

    def scatter_start(c, j):
        half = crows >> (j + 1)
        sbuf[c // SPLIT, slot(c, j), :] = acc[c // SPLIT, at_rows(drop[c][j], half), :].astype(BF16)
        scatter(c, j).start()

    def scatter_finish(c, j):
        half = crows >> (j + 1)
        scatter(c, j).wait_recv()
        mine = at_rows(keep[c][j], half)
        acc[c // SPLIT, mine, :] = acc[c // SPLIT, mine, :] + rbuf[c // SPLIT, slot(c, j), :].astype(F32)

    def gather(c, j):
        mine = at_rows(keep[c][j], crows >> (j + 1))
        return pltpu.make_async_remote_copy(
            src_ref=cand.at[c // SPLIT, mine, :], dst_ref=cand.at[c // SPLIT, mine, :],
            send_sem=ag_send.at[c, j], recv_sem=ag_recv.at[c, j],
            device_id={"ctx": partner[c][j]}, device_id_type=MESH)

    def gather_wait(c, j):
        theirs = at_rows(drop[c][j], crows >> (j + 1))
        pltpu.make_async_remote_copy(
            src_ref=cand.at[c // SPLIT, theirs, :], dst_ref=cand.at[c // SPLIT, theirs, :],
            send_sem=ag_send.at[c, j], recv_sem=ag_recv.at[c, j],
            device_id={"ctx": partner[c][j]}, device_id_type=MESH).wait_recv()

    def doc_setup():
        for load in doc_loads:
            load.wait()
        doc_cols[...] = as_column(doc_row()[:, win:])

    def doc_row():
        pick = lax.broadcasted_iota(jnp.int32, docs.shape, 0) == seq
        return jnp.sum(jnp.where(pick, docs[...], 0), axis=0, keepdims=True).astype(F32)

    def attend(i):
        at = block_at(i)
        span = win + BLOCK
        kb = kx[pl.ds(i * BLOCK, span), :]
        scores = lax.dot_general(
            q[at, :], kb, (((1,), (1,)), ((), ())), preferred_element_type=F32
        ) * (1.0 / math.sqrt(width))
        qpos = lax.broadcasted_iota(jnp.int32, scores.shape, 0) + win
        kpos = lax.broadcasted_iota(jnp.int32, scores.shape, 1)
        first = win - offset - i * BLOCK
        valid = (
            (kpos <= qpos) & (kpos > qpos - win) & (kpos >= first)
            & (doc_row()[:, i * BLOCK:i * BLOCK + span] == doc_cols[at, :][:, :1])
        )
        scores = jnp.where(valid, scores, -1e30)
        top = jnp.max(scores, axis=1, keepdims=True)
        expo = jnp.exp(scores - top)
        norm = 1.0 / jnp.sum(expo, axis=1, keepdims=True)
        probs = expo.astype(BF16)
        here = max(win - i * BLOCK, 0)
        y[at, :] = jnp.dot(
            probs[:, here:], vx[pl.ds(i * BLOCK + here, span - here), :],
            preferred_element_type=F32) * norm
        if here:
            held[i, :, 0:here] = probs[:, 0:here]
            norms[i] = jnp.broadcast_to(norm, norms.shape[1:])

    def rest(i):
        at = block_at(i)
        here = win - i * BLOCK

        @pl.when(me > 0)
        def _():
            for p in range(PIECES):
                if p * piece >= i * BLOCK and p not in arrived:
                    halo[1][p].wait_recv()
                    arrived.append(p)
        y[at, :] = y[at, :] + jnp.dot(
            held[i, :, 0:here], vx[pl.ds(i * BLOCK, here), :],
            preferred_element_type=F32) * norms[i][:, :1]

    def keys_wait():
        @pl.when(me > 0)
        def _():
            for p in range(PIECES):
                halo[0][p].wait_recv()

    def prepare(c):
        mom_loads[c].wait()
        old = jnp.transpose(w[c // SPLIT, :, lanes_own[c]].astype(F32), (1, 0))
        base[c] = old - 0.9 * jnp.transpose(mom[c], (1, 0))
        rms = jnp.sqrt(jnp.mean(old * old, axis=1, keepdims=True) + 1e-06)
        old_rms[c] = jnp.broadcast_to(rms, old_rms.shape[1:])

    def renew(c):
        mine = at_rows(low[c], own)
        part = base[c, within[c], :] - acc[c // SPLIT, mine, :]
        ratio = old_rms[c, within[c], :][:, :1] * lax.rsqrt(
            jnp.mean(part * part, axis=1, keepdims=True) + 1e-06)
        cand[c // SPLIT, mine, :] = (part * ratio).astype(BF16)

    taken = [0] * chunks

    def advance(c):
        step = taken[c]
        if step == 2 * phases:
            return
        taken[c] += 1
        if step < phases:
            scatter_finish(c, step)
            if step + 1 < phases:
                scatter_start(c, step + 1)
            else:
                renew(c)
                gather(c, phases - 1).start()
        else:
            j = 2 * phases - 1 - step
            gather_wait(c, j)
            if j > 0:
                gather(c, j - 1).start()

    def finish(c, upto):
        while taken[c] < upto:
            advance(c)

    across = (((0,), (0,)), ((), ()))
    nt = (((1,), (1,)), ((), ()))

    def hcols(h):
        return pl.ds(h * crows, crows)

    def gradient(c):
        right = u[...] if c // SPLIT == 2 else kx[pl.ds(win, rows), :]
        cols = hcols(c % SPLIT)
        acc[c // SPLIT, cols, :] = lax.dot_general(
            dh[c // SPLIT, :, cols], right, across, preferred_element_type=F32)
        scatter_start(c, 0)

    def back(h):
        if h == 0:
            w_loads[2].wait()
        cols = hcols(h)
        for i in range(0, rows, QBLOCK):
            at = pl.ds(i, QBLOCK)
            dg = jnp.dot(u[at, :], w[2, :, cols], preferred_element_type=F32)
            dh[0, at, cols] = (dg * hold[0, at, cols]).astype(BF16)
            dh[1, at, cols] = (dg * hold[1, at, cols]).astype(BF16)

    def gate(h):
        finish(h, 2 * phases)
        cols = hcols(h)
        for i in range(0, rows, QBLOCK):
            at = pl.ds(i, QBLOCK)
            o1 = lax.dot_general(q[at, :], cand[0, cols, :], nt, preferred_element_type=F32)
            hold[0, at, cols] = o1 / (1.0 + jnp.exp(-o1))

    def mix(h):
        finish(SPLIT + h, 2 * phases)
        cols = hcols(h)
        for i in range(0, rows, QBLOCK):
            at = pl.ds(i, QBLOCK)
            o3 = lax.dot_general(q[at, :], cand[1, cols, :], nt, preferred_element_type=F32)
            gq[at, cols] = (hold[0, at, cols] * o3).astype(BF16)

    def product(at, h):
        return jnp.dot(gq[at, hcols(h)], cand[2, hcols(h), :], preferred_element_type=F32)

    def down(h):
        finish(2 * SPLIT + h, 2 * phases)
        for i in range(0, rows, QBLOCK):
            at = pl.ds(i, QBLOCK)
            y[at, :] = y[at, :] + product(at, h)

    def turn(c):
        wt[c] = jnp.transpose(cand[c], (1, 0))

    early = [i for i in range(blocks) if i * BLOCK >= win]
    late = [i for i in range(blocks) if i * BLOCK < win][::-1]
    final = early + late
    rests = list(late)
    steps = {
        "F": forward, "|": meet, "K": keys_wait, "D": doc_setup, "Q": q_load.wait,
        "E": lambda: attend(early.pop(0)), "S": lambda: attend(late.pop(0)),
        "r": lambda: rest(rests.pop(0)),
        "V": lambda: halo_start(1, pieces.pop(0)),
    }
    pieces = list(range(PIECES))[::-1]
    arrived = []
    for c in range(chunks):
        steps[f"g{c}"] = functools.partial(gradient, c)
        steps[f"P{c}"] = functools.partial(prepare, c)
        steps[f"{c}"] = functools.partial(advance, c)
    for h in range(SPLIT):
        steps[f"B{h}"] = functools.partial(back, h)
        steps[f"O{h}"] = functools.partial(gate, h)
        steps[f"M{h}"] = functools.partial(mix, h)
        steps[f"W{h}"] = functools.partial(down, h)
    for num, step in enumerate(PLAN):
        with jax.named_scope(f"st{num:02d}_{step}"):
            steps[step]()

    def squares_copy(d, i):
        return pltpu.make_async_remote_copy(
            src_ref=ss_own.at[i], dst_ref=ss_got.at[d, i],
            send_sem=ss_send.at[d, i], recv_sem=ss_recv.at[d, i],
            device_id={"hs": peers[d]}, device_id_type=MESH)

    with jax.named_scope("last"):
        finish(chunks - 1, 2 * phases)
    for i in final:
        with jax.named_scope(f"fwb{i}"):
            at = block_at(i)
            mixed = y[at, :] + product(at, SPLIT - 1)
            y[at, :] = mixed
            sq = mixed * mixed
            lanes = sq[:, 0:128]
            for s in range(1, width // 128):
                lanes = lanes + sq[:, s * 128:(s + 1) * 128]
            row = jnp.sum(jnp.transpose(lanes, (1, 0)), axis=0, keepdims=True)
            ss_own[i] = jnp.broadcast_to(row, ss_own.shape[1:])
            for d in range(len(peers)):
                squares_copy(d, i).start()
    with jax.named_scope("turn2"):
        for c in range(3):
            turn(c)
    with jax.named_scope("sends"):
        gain_load.wait()
        for c in range(chunks):
            for j in range(phases):
                scatter(c, j).wait_send()
                gather(c, j).wait_send()

        @pl.when(me < n - 1)
        def _():
            for i in range(2):
                for p in range(PIECES):
                    halo[i][p].wait_send()

    for i in final:
        with jax.named_scope(f"ss{i}"):
            part = ss_own[i]
            for d in range(len(peers)):
                squares_copy(d, i).wait_recv()
                part = part + ss_got[d, i]
            ss_out[i] = part
            for d in range(len(peers)):
                squares_copy(d, i).wait_send()


def finale(count, y, ss, gain_ref, wt, out_hbm, new_hbm, outbuf, out_sem):
    rows, width = y.shape
    blocks = rows // BLOCK
    moves = [pltpu.make_async_copy(wt.at[c], new_hbm.at[c], out_sem.at[c]) for c in range(3)]
    for i in range(blocks):
        at = pl.ds(i * BLOCK, BLOCK)
        moves.append(pltpu.make_async_copy(outbuf.at[at], out_hbm.at[at], out_sem.at[3 + i]))
    for c in range(3):
        moves[c].start()
    gain = gain_ref[...]
    for i in range(blocks):
        at = pl.ds(i * BLOCK, BLOCK)
        scale = lax.rsqrt(as_column(ss[i][0:1, :]) * (1.0 / count) + 1e-06)
        for s in range(width // 128):
            cols = slice(s * 128, (s + 1) * 128)
            outbuf[at, cols] = (y[at, cols] * scale * gain[:, cols]).astype(BF16)
        moves[3 + i].start()
    for move in moves:
        move.wait()


def per_device(n, hs_count, queries, keys, values, rates, doc_ids, fast_weights, momentum, head_gain):
    rows, width = queries.shape[1:]
    _, mats, wrows, wcols = fast_weights.shape
    seqs = doc_ids.shape[0]
    heads = hs_count // seqs
    phases = n.bit_length() - 1
    blocks = rows // BLOCK
    ext = rows + WINDOW_TOKENS
    others = max(heads - 1, 1)
    any_spec = pl.BlockSpec(memory_space=pl.ANY)
    vmem = pl.BlockSpec(memory_space=pltpu.VMEM)
    dma = pltpu.SemaphoreType.DMA
    mixed, turned, squares, gain = pl.pallas_call(
        functools.partial(kernel, n, heads, seqs),
        out_shape=(
            pltpu.VMEM((rows, width), F32),
            pltpu.VMEM((mats, wrows, wcols), BF16),
            pltpu.VMEM((blocks, 8, BLOCK), F32),
            pltpu.VMEM((1, width), F32),
        ),
        in_specs=[any_spec] * 8,
        out_specs=(vmem,) * 4,
        scratch_shapes=[
            pltpu.VMEM((rows, width), BF16),
            pltpu.VMEM((ext, width), BF16),
            pltpu.VMEM((ext, width), BF16),
            pltpu.VMEM((mats, wrows, wcols), BF16),
            pltpu.VMEM((SPLIT * mats, wrows, 128), F32),
            pltpu.VMEM((seqs, ext), jnp.int32),
            pltpu.VMEM((1, rows), F32),
            pltpu.VMEM((mats, rows, wcols), BF16),
            pltpu.VMEM((rows, width), BF16),
            pltpu.VMEM((mats, wrows, wcols), F32),
            pltpu.VMEM((mats, wrows, wcols), BF16),
            pltpu.VMEM((mats, wrows, wcols), BF16),
            pltpu.VMEM((mats, wrows, wcols), BF16),
            pltpu.VMEM((SPLIT * mats, 128, wrows), F32),
            pltpu.VMEM((SPLIT * mats, 128, 128), F32),
            pltpu.VMEM((2, rows, wcols), F32),
            pltpu.VMEM((rows, wcols), BF16),
            pltpu.VMEM((WINDOW_TOKENS // BLOCK, BLOCK, WINDOW_TOKENS), BF16),
            pltpu.VMEM((WINDOW_TOKENS // BLOCK, BLOCK, 128), F32),
            pltpu.VMEM((blocks, 8, BLOCK), F32),
            pltpu.VMEM((others, blocks, 8, BLOCK), F32),
            pltpu.VMEM((rows, 128), F32),
            dma((blocks,)), dma((blocks,)), dma((3,)), dma((5 + SPLIT * mats,)), dma((2, PIECES)), dma((2, PIECES)),
            dma((SPLIT * mats, phases)), dma((SPLIT * mats, phases)),
            dma((SPLIT * mats, phases)), dma((SPLIT * mats, phases)),
            dma((others, blocks)), dma((others, blocks)),
        ],
        compiler_params=pltpu.CompilerParams(
            collective_id=0, has_side_effects=True, vmem_limit_bytes=48 * 1024 * 1024),
        name="lact_block",
    )(*[pltpu.with_memory_space_constraint(x, pltpu.HBM) for x in (
        queries[0], keys[0], values[0], rates, doc_ids, fast_weights[0], momentum[0], head_gain)])
    out, fresh = pl.pallas_call(
        functools.partial(finale, heads * width),
        out_shape=(
            jax.ShapeDtypeStruct((rows, width), BF16),
            jax.ShapeDtypeStruct((mats, wrows, wcols), BF16),
        ),
        in_specs=[vmem] * 4,
        out_specs=(any_spec, any_spec),
        scratch_shapes=[pltpu.VMEM((rows, width), BF16), dma((3 + blocks,))],
        compiler_params=pltpu.CompilerParams(vmem_limit_bytes=16 * 1024 * 1024),
        name="lact_finish",
    )(mixed, squares, gain, turned)
    return out[None], fresh[None]


def solution(mesh):
    return jax.shard_map(
        functools.partial(per_device, mesh.shape["ctx"], mesh.shape["hs"]),
        mesh=mesh,
        in_specs=(
            P("hs", "ctx", None),
            P("hs", "ctx", None),
            P("hs", "ctx", None),
            P("hs", "ctx"),
            P(),
            P("hs", None, None, None),
            P("hs", None, None, None),
            P("hs", None),
        ),
        out_specs=(P("hs", "ctx", None), P("hs", None, None, None)),
        check_vma=False,
    )
```
